32 devices in a mesh: week: 2 (over y), slab: 4 (over z), trank: 2 (over x), lrank: 2 (over core).
Axes of the slice: x: 2, y: 2, z: 4, core: 2. Of those that a mesh axis runs over, the one named last changes fastest.
Arguments:
- tiles: bfloat16 [1024, 4096], P(('week', 'slab', 'trank', 'lrank')), parts along dimension 0, may hold values from -6 to 6
- tile_var: int32 [1024], P(('week', 'slab', 'trank', 'lrank')), parts along dimension 0, may hold values from 0 to 5
- tile_time: int32 [1024], P(('week', 'slab', 'trank', 'lrank')), parts along dimension 0, may hold values from 0 to 127
- tile_level: int32 [1024], P(('week', 'slab', 'trank', 'lrank')), parts along dimension 0, may hold values from 0 to 47
- tile_block: int32 [1024], P(('week', 'slab', 'trank', 'lrank')), parts along dimension 0, may hold values from 0 to 63
- counts: int32 [32, 4], P(('week', 'slab', 'trank', 'lrank')), parts along dimension 0, may hold values from 0 to 8, as said below
- time_factor: bfloat16 [16, 256], P('week'), parts along dimension 0, may hold values from -0.5 to 0.5
- level_factor: bfloat16 [16, 96], P('week'), parts along dimension 0, may hold values from -0.875 to 0.875
- lat_factor: bfloat16 [64, 512], P('week'), parts along dimension 0, may hold values from -0.75 to 0.75
- lon_factor: bfloat16 [96, 2048], P(('week', 'slab')), parts along dimension 0, may hold values from -0.75 to 0.75
Outputs:
- grid: bfloat16 [96, 32, 384], P(('week', 'slab'), ('trank', 'lrank')), parts along dimension 0
The draws below stay inside these ranges and needn't reach their ends.
There are 2 independent parts, one for each index of `week`. The reference program is written for one: setup_inputs(seed, part) draws one part's arguments, and reference() takes and returns one part's arrays. A program takes and returns all parts, laid end to end along the dimension named above; each array names one. Nothing has to cross between parts.
Inputs may be any that keep to these rules, and one draw needn't show every extreme that they name: counts[i, e] is the number of live slots among the 8 slots for destination slab e of device row i; for every trank and lrank index some destination slab gets 8 live slots from every source slab.
All inputs are finite; a program needn't handle non-finite values.
Results may differ from the reference program's by a relative error of at most 0.0069.
Values may be sent and summed in bfloat16 or wider, within the bound.
A program may use at most 64 MiB of HBM per device.

```python
import jax
import jax.numpy as jnp
from jax import lax

V = 6
RT = 256
RL = 96
RC = 512
RD = 2048
BLK = 64
T_OUT = 8
L_OUT = 8
CAP = 8
SLABS = 4
GROUPS = 4
ROWS = 512
LATS = 32
LONS = 48
N_SLAB = 4
N_TRANK = 2
N_LRANK = 2


def draw_counts(key, part):
    key_hot, key_level, key_raw = jax.random.split(key, 3)
    hottest = jax.random.randint(key_hot, (GROUPS,), 0, SLABS)
    levels = jax.random.randint(key_level, (GROUPS, SLABS), 1, 5)
    raw_draw = jax.random.randint(key_raw, (SLABS, GROUPS, SLABS), 0, 1 << 20)
    limits = levels * CAP // 4 + 1
    drawn = raw_draw % limits[None, :, :]
    targets = jnp.arange(SLABS, dtype=jnp.int32)
    filled = targets[None, :] == hottest[:, None]
    drawn = jnp.where(filled[None, :, :], CAP, drawn)
    return drawn.reshape(SLABS * GROUPS, SLABS).astype(jnp.int32)


def plant(values, key, low, top_value):
    spot = [jax.random.randint(jax.random.fold_in(key, axis), (), 0, length) for axis, length in enumerate(values.shape)]
    longest = values.shape.index(max(values.shape))
    next_to = spot[:longest] + [(spot[longest] + 1) % values.shape[longest]] + spot[longest + 1:]
    return values.at[tuple(spot)].set(low).at[tuple(next_to)].set(top_value)


def shard_levels(stream_key, dims, pieces, least, high):
    def one(dim, blocks):
        heights = jax.random.uniform(jax.random.fold_in(jax.random.fold_in(stream_key, 6), dim), (blocks,), jnp.float32, least / len(pieces), high / len(pieces))
        return jnp.repeat(jnp.exp(heights), dims[dim] // blocks).reshape((-1,) + (1,) * (len(dims) - dim - 1))

    factor_of = one(*pieces[0])
    for cut in pieces[1:]:
        factor_of = factor_of * one(*cut)
    return factor_of


def normal_values(own_key, dims, scale, most, pieces=(), kind=jnp.bfloat16):
    result = jax.random.normal(own_key, dims, jnp.float32) * scale
    if len(pieces) > 0:
        result = shard_levels(own_key, dims, pieces, -0.22, 0.18) * result
    return jnp.clip(result, min=-most, max=most).astype(kind)


def setup_inputs(seed: int = 0, part: int = 0) -> dict:
    key_of = jax.random.split(jax.random.key(seed), 11)
    own_keys = jax.random.split(jax.random.fold_in(key_of[10], part), 11)
    tiles = normal_values(own_keys[0], (ROWS, BLK * BLK), 1.0, 6.0, ((0, 16),))
    tile_var = plant(jax.random.randint(own_keys[1], (ROWS,), 0, V), jax.random.fold_in(own_keys[1], 1), 0, V - 1).astype(jnp.int32)
    tile_time = plant(jax.random.randint(own_keys[2], (ROWS,), 0, RT // N_TRANK), jax.random.fold_in(own_keys[2], 1), 0, (RT // N_TRANK) - 1).astype(jnp.int32)
    tile_level = plant(jax.random.randint(own_keys[3], (ROWS,), 0, RL // N_LRANK), jax.random.fold_in(own_keys[3], 1), 0, (RL // N_LRANK) - 1).astype(jnp.int32)
    tile_block = plant(jax.random.randint(own_keys[4], (ROWS,), 0, (RC // BLK) * (RD // (BLK * N_SLAB))), jax.random.fold_in(own_keys[4], 1), 0, ((RC // BLK) * (RD // (BLK * N_SLAB))) - 1).astype(jnp.int32)
    counts = draw_counts(jax.random.fold_in(jax.random.fold_in(key_of[10], part), 71), part)
    time_factor = normal_values(own_keys[6], (T_OUT, RT), (RT // N_TRANK) ** -0.5, 0.5)
    level_factor = normal_values(own_keys[7], (L_OUT, RL), (RL // N_LRANK) ** -0.5, 0.875)
    lat_factor = normal_values(own_keys[8], (LATS, RC), BLK ** -0.5, 0.75)
    lon_factor = normal_values(own_keys[9], (LONS, RD), BLK ** -0.5, 0.75, ((0, 4),))
    return {"tiles": tiles, "tile_var": tile_var, "tile_time": tile_time, "tile_level": tile_level, "tile_block": tile_block, "counts": counts, "time_factor": time_factor, "level_factor": level_factor, "lat_factor": lat_factor, "lon_factor": lon_factor}


def reference(tiles, tile_var, tile_time, tile_level, tile_block, counts, time_factor, level_factor, lat_factor, lon_factor):
    groups = N_TRANK * N_LRANK
    time_dev = RT // N_TRANK
    level_dev = RL // N_LRANK
    dblocks = RD // (BLK * N_SLAB)
    cblocks = RC // BLK
    lat_rows = lat_factor.shape[0]
    fields = V * T_OUT * L_OUT
    lat_blocks = lat_factor.astype(jnp.float32).reshape(lat_rows, cblocks, BLK)
    tiles_all = tiles.reshape(N_SLAB, groups, N_SLAB, CAP, BLK, BLK)
    var_all = tile_var.reshape(N_SLAB, groups, N_SLAB, CAP)
    time_all = tile_time.reshape(N_SLAB, groups, N_SLAB, CAP)
    level_all = tile_level.reshape(N_SLAB, groups, N_SLAB, CAP)
    block_all = tile_block.reshape(N_SLAB, groups, N_SLAB, CAP)
    count_all = counts.reshape(N_SLAB, groups, N_SLAB)
    total_rows = N_SLAB * CAP

    def step(total, index):
        group = index // N_SLAB
        dest = index % N_SLAB
        block_tiles = tiles_all[:, group, dest].reshape(total_rows, BLK, BLK).astype(jnp.float32)
        variable = var_all[:, group, dest].reshape(total_rows)
        rank_time = time_all[:, group, dest].reshape(total_rows)
        rank_level = level_all[:, group, dest].reshape(total_rows)
        blocks = block_all[:, group, dest].reshape(total_rows)
        live = (jnp.arange(CAP, dtype=jnp.int32)[None, :] < count_all[:, group, dest][:, None]).reshape(total_rows)
        lat_index = blocks // dblocks
        lon_index = blocks % dblocks
        chosen = jnp.take(lat_blocks, lat_index, axis=1)
        partial_value = jnp.einsum('lrc,rcd->rld', chosen, block_tiles).astype(jnp.bfloat16)
        time_start = (group // N_LRANK) * time_dev
        level_start = (group % N_LRANK) * level_dev
        time_local = lax.dynamic_slice_in_dim(time_factor, time_start, time_dev, 1)
        level_local = lax.dynamic_slice_in_dim(level_factor, level_start, level_dev, 1)
        time_cols = jnp.take(time_local, rank_time, axis=1).T.astype(jnp.float32)
        level_cols = jnp.take(level_local, rank_level, axis=1).T.astype(jnp.float32)
        var_hot = (variable[:, None] == jnp.arange(V, dtype=jnp.int32)[None, :]).astype(jnp.float32)
        coef = var_hot[:, :, None, None] * time_cols[:, None, :, None] * level_cols[:, None, None, :]
        coef = (coef * live.astype(jnp.float32)[:, None, None, None]).reshape(total_rows, fields).astype(jnp.bfloat16)
        place = (lon_index[:, None] == jnp.arange(dblocks, dtype=jnp.int32)[None, :]).astype(jnp.float32)
        spread = partial_value.astype(jnp.float32)[:, :, None, :] * place[:, None, :, None]
        spread = spread.reshape(total_rows, lat_rows * dblocks * BLK)
        piece = jnp.einsum('rz,rx->zx', spread, coef.astype(jnp.float32))
        piece = lax.optimization_barrier(piece.astype(jnp.bfloat16)).astype(jnp.float32)
        piece = piece.reshape(lat_rows, dblocks * BLK, fields)
        return total.at[dest].add(piece), None

    start = jnp.zeros((N_SLAB, lat_rows, dblocks * BLK, fields), jnp.float32)
    total, _ = lax.scan(step, start, jnp.arange(groups * N_SLAB, dtype=jnp.int32))
    core_image = jnp.transpose(total, (1, 0, 2, 3)).reshape(lat_rows, RD, fields).astype(jnp.bfloat16)
    grid = jnp.einsum('od,ldx->olx', lon_factor.astype(jnp.float32), core_image.astype(jnp.float32))
    return grid.astype(jnp.bfloat16)
```

```python
import functools

import jax
import jax.numpy as jnp
from jax import lax
from jax.experimental import pallas as pl
from jax.experimental.pallas import tpu as pltpu
from jax.sharding import PartitionSpec as P

V = 6
RT = 256
RL = 96
RC = 512
RD = 2048
BLK = 64


def general_plan(
    tiles,
    tile_var,
    tile_time,
    tile_level,
    tile_block,
    counts,
    time_factor,
    level_factor,
    lat_factor,
    lon_factor,
):
    slabs = lax.axis_size("slab")
    n_trank = lax.axis_size("trank")
    n_lrank = lax.axis_size("lrank")
    slots = tiles.shape[0]
    capacity = slots // slabs
    lat_rows = lat_factor.shape[0]
    cblocks = RC // BLK
    dblocks = RD // (BLK * slabs)
    time_dev = RT // n_trank
    level_dev = RL // n_lrank
    hours = time_factor.shape[0]
    levels = level_factor.shape[0]
    fields = V * hours * levels
    lat_blocks = lat_factor.reshape(lat_rows, cblocks, BLK)
    sent_counts = counts.reshape(slabs)
    slot_index = jnp.arange(slots, dtype=jnp.int32)
    live_sent = (slot_index % capacity < jnp.repeat(sent_counts, capacity)).astype(jnp.int32)
    got_tiles, variable, rank_time, rank_level, blocks, live_got = (
        lax.all_to_all(tiles, "slab", split_axis=0, concat_axis=0, tiled=True),
        lax.all_to_all(tile_var, "slab", split_axis=0, concat_axis=0, tiled=True),
        lax.all_to_all(tile_time, "slab", split_axis=0, concat_axis=0, tiled=True),
        lax.all_to_all(tile_level, "slab", split_axis=0, concat_axis=0, tiled=True),
        lax.all_to_all(tile_block, "slab", split_axis=0, concat_axis=0, tiled=True),
        lax.all_to_all(live_sent, "slab", split_axis=0, concat_axis=0, tiled=True),
    )
    chosen = jnp.take(lat_blocks, blocks // dblocks, axis=1)
    square = got_tiles.reshape(got_tiles.shape[0], BLK, BLK)
    product = jnp.einsum("lkc,kcd->kld", chosen, square, preferred_element_type=jnp.float32)
    partial_value = product.astype(jnp.bfloat16)
    time_full = lax.axis_index("trank") * time_dev + rank_time
    level_full = lax.axis_index("lrank") * level_dev + rank_level
    var_hot = (variable[:, None] == jnp.arange(V, dtype=jnp.int32)[None, :]).astype(jnp.float32)
    time_cols = jnp.take(time_factor, time_full, axis=1).T.astype(jnp.float32)
    level_cols = jnp.take(level_factor, level_full, axis=1).T.astype(jnp.float32)
    coef = var_hot[:, :, None, None] * time_cols[:, None, :, None] * level_cols[:, None, None, :]
    coef = coef * live_got.astype(jnp.float32)[:, None, None, None]
    coef = coef.reshape(variable.shape[0], fields).astype(jnp.bfloat16)
    place = (blocks % dblocks)[:, None] == jnp.arange(dblocks, dtype=jnp.int32)[None, :]
    spread_spread = jnp.where(
        place[:, None, :, None], partial_value[:, :, None, :], jnp.zeros((), jnp.bfloat16)
    )
    spread = spread_spread.reshape(partial_value.shape[0], partial_value.shape[1], dblocks * BLK)
    summed = lax.psum_scatter(
        jnp.einsum("kld,kx->ldx", spread, coef, preferred_element_type=jnp.float32).astype(
            jnp.bfloat16
        ),
        ("trank", "lrank"),
        scatter_dimension=0,
        tiled=True,
    )
    grid = jnp.einsum(
        "od,ldx->olx",
        lon_factor,
        lax.all_gather(summed, "slab", axis=1, tiled=True),
        preferred_element_type=jnp.float32,
    )
    return grid.astype(jnp.bfloat16)


LANES = 128
MESH = pl.DeviceIdType.MESH


def offsets(shape):
    slabs, tranks, lranks = shape
    found = [
        (a, b, c)
        for a in range(slabs)
        for b in range(tranks)
        for c in range(lranks)
        if (a, b, c) != (0, 0, 0)
    ]
    return sorted(found, key=lambda k: -(min(k[0], slabs - k[0]) * 4 + k[1] * 2 + k[2]))


def decode_kernel(
    shape,
    tiles_ref,
    var_ref,
    time_ref,
    level_ref,
    blk_ref,
    counts_ref,
    time_factor_ref,
    level_factor_ref,
    lat_ref,
    lon_ref,
    out_ref,
    square,
    lat_blocks,
    partials,
    lon_mine,
    lon_all,
    weights,
    send_buf,
    recv_buf,
    meta_mine,
    meta_all,
    coef,
    result,
    lon_send,
    lon_recv,
    meta_send,
    meta_recv,
    w_send,
    w_recv,
):
    slabs, tranks, lranks = shape
    groups = tranks * lranks
    devices = slabs * groups
    week = lax.axis_index("week")
    slab = lax.axis_index("slab")
    trank = lax.axis_index("trank")
    lrank = lax.axis_index("lrank")
    me = slab * groups + trank * lranks + lrank
    rows = tiles_ref.shape[0]
    capacity = rows // slabs
    lats = lat_ref.shape[0]
    lat_dev = lats // groups
    lons, lon_pad = lon_ref.shape[0], lon_mine.shape[0]
    depth = RD // slabs
    dblocks = depth // BLK
    per_lane = LANES // BLK
    hours = time_factor_ref.shape[0]
    levels = level_factor_ref.shape[0]
    time_dev = RT // tranks
    level_dev = RL // lranks
    total_rows = rows * devices
    pieces = offsets(shape)

    def peer(k):
        a, b, c = k
        return (
            lax.rem(slab + a, slabs),
            lax.rem(trank + b, tranks),
            lax.rem(lrank + c, lranks),
        )

    lon_mine[...] = jnp.concatenate(
        [lon_ref[...].astype(jnp.float32), jnp.zeros((lon_pad - lons, RD), jnp.float32)], axis=0
    ).astype(jnp.bfloat16)
    lane = lax.broadcasted_iota(jnp.int32, (1, rows), 1)
    live = jnp.zeros((1, rows), jnp.int32)
    for e in range(slabs):
        first = e * capacity
        live = jnp.where((lane >= first) & (lane < first + counts_ref[0, e]), 1, live)
    meta_mine[...] = jnp.concatenate(
        [
            var_ref[...],
            time_ref[...] + trank * time_dev,
            level_ref[...] + lrank * level_dev,
            live,
        ],
        axis=1,
    )
    barrier = pltpu.get_barrier_semaphore()
    for k in pieces:
        pl.semaphore_signal(barrier, inc=1, device_id=(week, *peer(k)), device_id_type=MESH)
    pl.semaphore_wait(barrier, devices - 1)

    lon_copies = []
    for a in sorted(range(1, slabs), key=lambda a: -min(a, slabs - a)):
        lon_copies.append(
            pltpu.make_async_remote_copy(
                src_ref=lon_mine,
                dst_ref=lon_all.at[slab],
                send_sem=lon_send.at[a],
                recv_sem=lon_recv.at[a],
                device_id=(week, lax.rem(slab + a, slabs), trank, lrank),
                device_id_type=MESH,
            )
        )
        lon_copies[-1].start()
    meta_copies = []
    for n, k in enumerate(pieces):
        meta_copies.append(
            pltpu.make_async_remote_copy(
                src_ref=meta_mine,
                dst_ref=meta_all.at[me],
                send_sem=meta_send.at[n],
                recv_sem=meta_recv.at[n],
                device_id=(week, *peer(k)),
                device_id_type=MESH,
            )
        )
        meta_copies[-1].start()
    lon_all[slab] = lon_mine[...]
    meta_all[me] = meta_mine[...]

    half = lax.broadcasted_iota(jnp.int32, (rows, LANES), 1) < BLK
    for j in range(BLK // per_lane):
        chunk = tiles_ref[:, j * LANES : (j + 1) * LANES].astype(jnp.float32)
        turned = pltpu.roll(chunk, BLK, 1)
        square[pl.ds(per_lane * j, rows, stride=BLK), :] = jnp.where(half, chunk, turned)
        square[pl.ds(per_lane * j + 1, rows, stride=BLK), :] = jnp.where(half, turned, chunk)
    for cb in range(RC // BLK):
        lat_blocks[cb] = lat_ref[:, cb * BLK : (cb + 1) * BLK]
    for r in range(rows):
        e, q = r // capacity, r % capacity
        partials[e, pl.ds(q, lats, stride=capacity), :] = jnp.dot(
            lat_blocks[blk_ref[r] // dblocks],
            square[r * BLK : (r + 1) * BLK, :].astype(jnp.bfloat16),
            preferred_element_type=jnp.float32,
        )

    for copy in meta_copies:
        copy.wait()

    def field(k):
        return jnp.concatenate(
            [meta_all[i][:, k * rows : (k + 1) * rows] for i in range(devices)], axis=1
        )

    variable, rank_time, rank_level, alive = field(0), field(1), field(2), field(3)
    time_hot = (
        lax.broadcasted_iota(jnp.int32, (RT, total_rows), 0) == rank_time
    ).astype(jnp.float32).astype(jnp.bfloat16)
    level_hot = (
        lax.broadcasted_iota(jnp.int32, (RL, total_rows), 0) == rank_level
    ).astype(jnp.float32).astype(jnp.bfloat16)
    time_f = time_factor_ref[...].astype(jnp.float32)
    time_rows = jnp.concatenate(
        [jnp.broadcast_to(time_f[t : t + 1], (levels, RT)) for t in range(hours)], axis=0
    ).astype(jnp.bfloat16)
    level_f = level_factor_ref[...].astype(jnp.float32)
    level_rows = jnp.concatenate([level_f] * hours, axis=0).astype(jnp.bfloat16)
    product = (
        jnp.dot(time_rows, time_hot, preferred_element_type=jnp.float32)
        * jnp.dot(level_rows, level_hot, preferred_element_type=jnp.float32)
        * alive.astype(jnp.float32)
    )
    per_var = hours * levels
    for v in range(V):
        coef[v * per_var : (v + 1) * per_var, :] = jnp.where(
            variable == v, product, 0.0
        ).astype(jnp.bfloat16)

    for copy in lon_copies:
        copy.wait()
    sub = lax.broadcasted_iota(jnp.int32, (capacity, LANES), 0)
    side = lax.broadcasted_iota(jnp.int32, (capacity, LANES), 1) // BLK
    for e in range(slabs):
        place = jnp.zeros((capacity, LANES), jnp.int32)
        for q in range(capacity):
            place = jnp.where(sub == q, blk_ref[e * capacity + q] % dblocks, place)
        part = partials[e].reshape(lats, capacity, LANES)
        spread = jnp.concatenate(
            [
                jnp.where((place == per_lane * b + side)[None], part, 0.0)
                for b in range(dblocks // per_lane)
            ],
            axis=2,
        ).reshape(lats * capacity, depth).astype(jnp.bfloat16)
        longitudes = lon_all[:, :, e * depth : (e + 1) * depth].reshape(slabs * lon_pad, depth)
        value = lax.dot_general(
            spread, longitudes, (((1,), (1,)), ((), ())), preferred_element_type=jnp.float32
        )
        weights[:, :, e * capacity : (e + 1) * capacity, :] = value.reshape(
            groups, lat_dev, capacity, slabs * lon_pad
        )
    for g in range(groups):
        turned = weights[g].reshape(lat_dev * rows, slabs * lon_pad).T
        send_buf[g] = turned.astype(jnp.bfloat16).reshape(slabs, lon_pad, lat_dev * rows)

    w_copies = []
    for n, k in enumerate(pieces):
        to_slab, to_trank, to_lrank = peer(k)
        w_copies.append(
            pltpu.make_async_remote_copy(
                src_ref=send_buf.at[to_trank * lranks + to_lrank, to_slab],
                dst_ref=recv_buf.at[me],
                send_sem=w_send.at[n],
                recv_sem=w_recv.at[n],
                device_id=(week, to_slab, to_trank, to_lrank),
                device_id_type=MESH,
            )
        )
        w_copies[-1].start()
    recv_buf[me] = send_buf[trank * lranks + lrank, slab]
    for copy in w_copies:
        copy.wait()

    got = [recv_buf[i].astype(jnp.float32) for i in range(devices)]
    left = jnp.concatenate(
        [
            jnp.concatenate([x[:, y * rows : (y + 1) * rows] for x in got], axis=1)
            for y in range(lat_dev)
        ],
        axis=0,
    ).astype(jnp.bfloat16)
    full = lax.dot_general(
        left, coef[...], (((1,), (1,)), ((), ())), preferred_element_type=jnp.float32
    )
    blocks = full.shape[1] // LANES
    for b in range(blocks):
        result[b] = full[:, b * LANES : (b + 1) * LANES]
    for o in range(lons):
        out_ref[o] = jnp.concatenate(
            [result[b, pl.ds(o, lat_dev, stride=lon_pad), :] for b in range(blocks)], axis=1
        ).astype(jnp.bfloat16)


def scratch_of(shape, tiles, lat_factor, lon_factor, fields):
    slabs, tranks, lranks = shape
    groups = tranks * lranks
    devices = slabs * groups
    rows = tiles.shape[0]
    lats, lons = lat_factor.shape[0], lon_factor.shape[0]
    lat_dev = lats // groups
    lon_pad = -(-lons // 16) * 16
    return [
        ((rows * BLK, LANES), jnp.float32),
        ((RC // BLK, lats, BLK), jnp.bfloat16),
        ((slabs, lats * (rows // slabs), LANES), jnp.float32),
        ((lon_pad, RD), jnp.bfloat16),
        ((slabs, lon_pad, RD), jnp.bfloat16),
        ((groups, lat_dev, rows, slabs * lon_pad), jnp.float32),
        ((groups, slabs, lon_pad, lat_dev * rows), jnp.bfloat16),
        ((devices, lon_pad, lat_dev * rows), jnp.bfloat16),
        ((1, 4 * rows), jnp.int32),
        ((devices, 1, 4 * rows), jnp.int32),
        ((fields, devices * rows), jnp.bfloat16),
        ((fields // LANES, lat_dev * lon_pad, LANES), jnp.float32),
    ]


def bytes_of(buffers):
    total = 0
    for dims, kind in buffers:
        size = jnp.dtype(kind).itemsize
        for d in dims[:-1]:
            size *= d
        total += size * (-(-dims[-1] // LANES) * LANES)
    return total


def per_device(
    tiles,
    tile_var,
    tile_time,
    tile_level,
    tile_block,
    counts,
    time_factor,
    level_factor,
    lat_factor,
    lon_factor,
):
    shape = tuple(lax.axis_size(name) for name in ("slab", "trank", "lrank"))
    slabs = shape[0]
    devices = shape[0] * shape[1] * shape[2]
    rows = tiles.shape[0]
    fields = V * time_factor.shape[0] * level_factor.shape[0]
    buffers = scratch_of(shape, tiles, lat_factor, lon_factor, fields)
    fits = (
        4 * rows == LANES
        and rows // slabs == 8
        and (RD // slabs) % LANES == 0
        and fields % LANES == 0
        and bytes_of(buffers) < (24 << 20)
    )
    if not fits:
        return general_plan(
            tiles,
            tile_var,
            tile_time,
            tile_level,
            tile_block,
            counts,
            time_factor,
            level_factor,
            lat_factor,
            lon_factor,
        )
    lat_dev = lat_factor.shape[0] // (devices // slabs)
    in_vmem = pl.BlockSpec(memory_space=pltpu.VMEM)
    in_smem = pl.BlockSpec(memory_space=pltpu.SMEM)
    return pl.pallas_call(
        functools.partial(decode_kernel, shape),
        out_shape=jax.ShapeDtypeStruct((lon_factor.shape[0], lat_dev, fields), jnp.bfloat16),
        in_specs=[in_vmem] * 4 + [in_smem] * 2 + [in_vmem] * 4,
        out_specs=in_vmem,
        scratch_shapes=[pltpu.VMEM(dims, kind) for dims, kind in buffers]
        + [pltpu.SemaphoreType.DMA((slabs,))] * 2
        + [pltpu.SemaphoreType.DMA((devices - 1,))] * 4,
        compiler_params=pltpu.CompilerParams(collective_id=0, has_side_effects=True),
        name="decode",
    )(
        tiles,
        tile_var.reshape(1, rows),
        tile_time.reshape(1, rows),
        tile_level.reshape(1, rows),
        tile_block,
        counts,
        time_factor,
        level_factor,
        lat_factor,
        lon_factor,
    )


def solution(mesh):
    in_specs = (
        P(("week", "slab", "trank", "lrank"), None),
        P(("week", "slab", "trank", "lrank")),
        P(("week", "slab", "trank", "lrank")),
        P(("week", "slab", "trank", "lrank")),
        P(("week", "slab", "trank", "lrank")),
        P(("week", "slab", "trank", "lrank"), None),
        P("week", None),
        P("week", None),
        P("week", None),
        P(("week", "slab"), None),
    )
    out_specs = P(("week", "slab"), ("trank", "lrank"), None)
    return jax.shard_map(
        per_device, mesh=mesh, in_specs=in_specs, out_specs=out_specs, check_vma=False
    )
```

```python
import functools

import jax
import jax.numpy as jnp
from jax import lax
from jax.experimental import pallas as pl
from jax.experimental.pallas import tpu as pltpu
from jax.sharding import PartitionSpec as P

V = 6
RT = 256
RL = 96
RC = 512
RD = 2048
BLK = 64


def general_plan(
    tiles,
    tile_var,
    tile_time,
    tile_level,
    tile_block,
    counts,
    time_factor,
    level_factor,
    lat_factor,
    lon_factor,
):
    slabs = lax.axis_size("slab")
    n_trank = lax.axis_size("trank")
    n_lrank = lax.axis_size("lrank")
    slots = tiles.shape[0]
    capacity = slots // slabs
    lat_rows = lat_factor.shape[0]
    cblocks = RC // BLK
    dblocks = RD // (BLK * slabs)
    time_dev = RT // n_trank
    level_dev = RL // n_lrank
    hours = time_factor.shape[0]
    levels = level_factor.shape[0]
    fields = V * hours * levels
    lat_blocks = lat_factor.reshape(lat_rows, cblocks, BLK)
    sent_counts = counts.reshape(slabs)
    slot_index = jnp.arange(slots, dtype=jnp.int32)
    live_sent = (slot_index % capacity < jnp.repeat(sent_counts, capacity)).astype(jnp.int32)
    got_tiles, variable, rank_time, rank_level, blocks, live_got = (
        lax.all_to_all(tiles, "slab", split_axis=0, concat_axis=0, tiled=True),
        lax.all_to_all(tile_var, "slab", split_axis=0, concat_axis=0, tiled=True),
        lax.all_to_all(tile_time, "slab", split_axis=0, concat_axis=0, tiled=True),
        lax.all_to_all(tile_level, "slab", split_axis=0, concat_axis=0, tiled=True),
        lax.all_to_all(tile_block, "slab", split_axis=0, concat_axis=0, tiled=True),
        lax.all_to_all(live_sent, "slab", split_axis=0, concat_axis=0, tiled=True),
    )
    chosen = jnp.take(lat_blocks, blocks // dblocks, axis=1)
    square = got_tiles.reshape(got_tiles.shape[0], BLK, BLK)
    product = jnp.einsum("lkc,kcd->kld", chosen, square, preferred_element_type=jnp.float32)
    partial_value = product.astype(jnp.bfloat16)
    time_full = lax.axis_index("trank") * time_dev + rank_time
    level_full = lax.axis_index("lrank") * level_dev + rank_level
    var_hot = (variable[:, None] == jnp.arange(V, dtype=jnp.int32)[None, :]).astype(jnp.float32)
    time_cols = jnp.take(time_factor, time_full, axis=1).T.astype(jnp.float32)
    level_cols = jnp.take(level_factor, level_full, axis=1).T.astype(jnp.float32)
    coef = var_hot[:, :, None, None] * time_cols[:, None, :, None] * level_cols[:, None, None, :]
    coef = coef * live_got.astype(jnp.float32)[:, None, None, None]
    coef = coef.reshape(variable.shape[0], fields).astype(jnp.bfloat16)
    place = (blocks % dblocks)[:, None] == jnp.arange(dblocks, dtype=jnp.int32)[None, :]
    spread_spread = jnp.where(
        place[:, None, :, None], partial_value[:, :, None, :], jnp.zeros((), jnp.bfloat16)
    )
    spread = spread_spread.reshape(partial_value.shape[0], partial_value.shape[1], dblocks * BLK)
    summed = lax.psum_scatter(
        jnp.einsum("kld,kx->ldx", spread, coef, preferred_element_type=jnp.float32).astype(
            jnp.bfloat16
        ),
        ("trank", "lrank"),
        scatter_dimension=0,
        tiled=True,
    )
    grid = jnp.einsum(
        "od,ldx->olx",
        lon_factor,
        lax.all_gather(summed, "slab", axis=1, tiled=True),
        preferred_element_type=jnp.float32,
    )
    return grid.astype(jnp.bfloat16)


LANES = 128
MESH = pl.DeviceIdType.MESH


def offsets(shape):
    slabs, tranks, lranks = shape
    found = [
        (a, b, c)
        for a in range(slabs)
        for b in range(tranks)
        for c in range(lranks)
        if (a, b, c) != (0, 0, 0)
    ]
    return sorted(found, key=lambda k: -(min(k[0], slabs - k[0]) * 4 + k[1] * 2 + k[2]))


def decode_kernel(
    shape,
    tiles_hbm,
    var_hbm,
    time_hbm,
    level_hbm,
    blk_hbm,
    counts_hbm,
    time_factor_hbm,
    level_factor_hbm,
    lat_hbm,
    lon_hbm,
    out_ref,
    square,
    lat_blocks,
    partials,
    stage,
    stage_place,
    got_part,
    got_place,
    lon_all,
    weights,
    send_buf,
    recv_buf,
    meta_mine,
    meta_all,
    coef,
    result,
    tiles_ref,
    index_ref,
    time_factor_ref,
    level_factor_ref,
    lat_ref,
    blk_ref,
    counts_ref,
    load_sem,
    lon_send,
    lon_recv,
    part_send,
    part_recv,
    place_send,
    place_recv,
    meta_send,
    meta_recv,
    w_send,
    w_recv,
):
    slabs, tranks, lranks = shape
    groups = tranks * lranks
    devices = slabs * groups
    week = lax.axis_index("week")
    slab = lax.axis_index("slab")
    trank = lax.axis_index("trank")
    lrank = lax.axis_index("lrank")
    me = slab * groups + trank * lranks + lrank
    rows = tiles_ref.shape[0]
    capacity = rows // slabs
    lats = lat_ref.shape[0]
    lat_dev = lats // groups
    lons, lon_pad = lon_hbm.shape[0], recv_buf.shape[1]
    own = slabs // lranks
    own_rows = own * capacity
    depth = RD // slabs
    dblocks = depth // BLK
    per_lane = LANES // BLK
    hours = time_factor_ref.shape[0]
    levels = level_factor_ref.shape[0]
    time_dev = RT // tranks
    level_dev = RL // lranks
    total_rows = rows * devices
    pieces = offsets(shape)

    def peer(k):
        a, b, c = k
        return (
            lax.rem(slab + a, slabs),
            lax.rem(trank + b, tranks),
            lax.rem(lrank + c, lranks),
        )

    barrier = pltpu.get_barrier_semaphore()
    for k in pieces:
        pl.semaphore_signal(barrier, inc=1, device_id=(week, *peer(k)), device_id_type=MESH)
    columns = pl.ds(pl.multiple_of(lrank * (own * depth), own * depth), own * depth)
    loads = [
        pltpu.make_async_copy(src, dst, load_sem.at[n])
        for n, (src, dst) in enumerate(
            [
                (tiles_hbm, tiles_ref),
                (lat_hbm, lat_ref),
                (blk_hbm, blk_ref),
                (counts_hbm, counts_ref),
                (var_hbm, index_ref.at[0]),
                (time_hbm, index_ref.at[1]),
                (level_hbm, index_ref.at[2]),
                (time_factor_hbm, time_factor_ref),
                (level_factor_hbm, level_factor_ref),
                (lon_hbm.at[:, columns], lon_all.at[slab]),
            ]
        )
    ]
    for load in loads:
        load.start()
    for load in loads:
        load.wait()

    lane = lax.broadcasted_iota(jnp.int32, (1, rows), 1)
    live = jnp.zeros((1, rows), jnp.int32)
    for e in range(slabs):
        first = e * capacity
        live = jnp.where((lane >= first) & (lane < first + counts_ref[0, e]), 1, live)
    meta_mine[...] = jnp.concatenate(
        [
            index_ref[0],
            index_ref[1] + trank * time_dev,
            index_ref[2] + lrank * level_dev,
            live,
        ],
        axis=1,
    )
    pl.semaphore_wait(barrier, devices - 1)

    lon_copies = []
    for a in sorted(range(1, slabs), key=lambda a: -min(a, slabs - a)):
        lon_copies.append(
            pltpu.make_async_remote_copy(
                src_ref=lon_hbm.at[:, columns],
                dst_ref=lon_all.at[slab],
                send_sem=lon_send.at[a],
                recv_sem=lon_recv.at[a],
                device_id=(week, lax.rem(slab + a, slabs), trank, lrank),
                device_id_type=MESH,
            )
        )
        lon_copies[-1].start()
    meta_copies = []
    for n, k in enumerate(pieces):
        meta_copies.append(
            pltpu.make_async_remote_copy(
                src_ref=meta_mine,
                dst_ref=meta_all.at[me],
                send_sem=meta_send.at[n],
                recv_sem=meta_recv.at[n],
                device_id=(week, *peer(k)),
                device_id_type=MESH,
            )
        )
        meta_copies[-1].start()
    meta_all[me] = meta_mine[...]

    half = lax.broadcasted_iota(jnp.int32, (rows, LANES), 1) < BLK
    for j in range(BLK // per_lane):
        chunk = tiles_ref[:, j * LANES : (j + 1) * LANES].astype(jnp.float32)
        turned = pltpu.roll(chunk, BLK, 1)
        square[pl.ds(per_lane * j, rows, stride=BLK), :] = jnp.where(half, chunk, turned)
        square[pl.ds(per_lane * j + 1, rows, stride=BLK), :] = jnp.where(half, turned, chunk)
    for cb in range(RC // BLK):
        lat_blocks[cb] = lat_ref[:, cb * BLK : (cb + 1) * BLK]
    for r in range(rows):
        e, q = r // capacity, r % capacity
        partials[e, pl.ds(q, lats, stride=capacity), :] = jnp.dot(
            lat_blocks[blk_ref[r] // dblocks],
            square[r * BLK : (r + 1) * BLK, :].astype(jnp.bfloat16),
            preferred_element_type=jnp.float32,
        )

    sub = lax.broadcasted_iota(jnp.int32, (capacity, LANES), 0)
    side = lax.broadcasted_iota(jnp.int32, (capacity, LANES), 1) // BLK
    for e in range(slabs):
        place = jnp.zeros((capacity, LANES), jnp.int32)
        for q in range(capacity):
            place = jnp.where(sub == q, blk_ref[e * capacity + q] % dblocks, place)
        stage_place[e] = place
    stage[...] = partials[...].astype(jnp.bfloat16)

    part_copies = []
    for c in range(1, lranks):
        other = lax.rem(lrank + c, lranks)
        theirs = pl.ds(other * own, own)
        for src, dst, send, recv in (
            (stage, got_part, part_send, part_recv),
            (stage_place, got_place, place_send, place_recv),
        ):
            part_copies.append(
                pltpu.make_async_remote_copy(
                    src_ref=src.at[theirs],
                    dst_ref=dst.at[lrank],
                    send_sem=send.at[c],
                    recv_sem=recv.at[c],
                    device_id=(week, slab, trank, other),
                    device_id_type=MESH,
                )
            )
            part_copies[-1].start()
    got_part[lrank] = stage[pl.ds(lrank * own, own)]
    got_place[lrank] = stage_place[pl.ds(lrank * own, own)]
    for copy in part_copies:
        copy.wait()

    for copy in lon_copies:
        copy.wait()
    blank = jnp.zeros((slabs, lon_pad - lons, depth), jnp.float32)
    for e in range(own):
        longitudes = jnp.concatenate(
            [lon_all[:, :, e * depth : (e + 1) * depth].astype(jnp.float32), blank], axis=1
        ).reshape(slabs * lon_pad, depth).astype(jnp.bfloat16)
        for source in range(lranks):
            place = got_place[source, e]
            part = got_part[source, e].astype(jnp.float32).reshape(lats, capacity, LANES)
            spread = jnp.concatenate(
                [
                    jnp.where((place == per_lane * b + side)[None], part, 0.0)
                    for b in range(dblocks // per_lane)
                ],
                axis=2,
            ).reshape(lats * capacity, depth).astype(jnp.bfloat16)
            value = lax.dot_general(
                spread, longitudes, (((1,), (1,)), ((), ())), preferred_element_type=jnp.float32
            )
            first = source * own_rows + e * capacity
            weights[:, :, first : first + capacity, :] = value.reshape(
                groups, lat_dev, capacity, slabs * lon_pad
            )
    for g in range(groups):
        turned = weights[g].reshape(lat_dev * rows, slabs * lon_pad).T
        send_buf[g] = turned.astype(jnp.bfloat16).reshape(slabs, lon_pad, lat_dev * rows)

    w_copies = []
    for n, k in enumerate(pieces):
        to_slab, to_trank, to_lrank = peer(k)
        w_copies.append(
            pltpu.make_async_remote_copy(
                src_ref=send_buf.at[to_trank * lranks + to_lrank, to_slab],
                dst_ref=recv_buf.at[me],
                send_sem=w_send.at[n],
                recv_sem=w_recv.at[n],
                device_id=(week, to_slab, to_trank, to_lrank),
                device_id_type=MESH,
            )
        )
        w_copies[-1].start()
    recv_buf[me] = send_buf[trank * lranks + lrank, slab]

    for copy in meta_copies:
        copy.wait()

    def field(k):
        return jnp.concatenate(
            [
                meta_all[p * lranks + source][
                    :, k * rows + core * own_rows : k * rows + (core + 1) * own_rows
                ]
                for p in range(devices // lranks)
                for core in range(lranks)
                for source in range(lranks)
            ],
            axis=1,
        )

    variable, rank_time, rank_level, alive = field(0), field(1), field(2), field(3)
    time_hot = (
        lax.broadcasted_iota(jnp.int32, (RT, total_rows), 0) == rank_time
    ).astype(jnp.float32).astype(jnp.bfloat16)
    level_hot = (
        lax.broadcasted_iota(jnp.int32, (RL, total_rows), 0) == rank_level
    ).astype(jnp.float32).astype(jnp.bfloat16)
    time_f = time_factor_ref[...].astype(jnp.float32)
    time_rows = jnp.concatenate(
        [jnp.broadcast_to(time_f[t : t + 1], (levels, RT)) for t in range(hours)], axis=0
    ).astype(jnp.bfloat16)
    level_f = level_factor_ref[...].astype(jnp.float32)
    level_rows = jnp.concatenate([level_f] * hours, axis=0).astype(jnp.bfloat16)
    product = (
        jnp.dot(time_rows, time_hot, preferred_element_type=jnp.float32)
        * jnp.dot(level_rows, level_hot, preferred_element_type=jnp.float32)
        * alive.astype(jnp.float32)
    )
    per_var = hours * levels
    for v in range(V):
        coef[v * per_var : (v + 1) * per_var, :] = jnp.where(
            variable == v, product, 0.0
        ).astype(jnp.bfloat16)

    for copy in w_copies:
        copy.wait()

    got = [recv_buf[i].astype(jnp.float32) for i in range(devices)]
    left = jnp.concatenate(
        [
            jnp.concatenate([x[:, y * rows : (y + 1) * rows] for x in got], axis=1)
            for y in range(lat_dev)
        ],
        axis=0,
    ).astype(jnp.bfloat16)
    full = lax.dot_general(
        left, coef[...], (((1,), (1,)), ((), ())), preferred_element_type=jnp.float32
    )
    blocks = full.shape[1] // LANES
    for b in range(blocks):
        result[b] = full[:, b * LANES : (b + 1) * LANES]
    for o in range(lons):
        out_ref[o] = jnp.concatenate(
            [result[b, pl.ds(o, lat_dev, stride=lon_pad), :] for b in range(blocks)], axis=1
        ).astype(jnp.bfloat16)


def scratch_of(shape, tiles, time_factor, level_factor, lat_factor, lon_factor):
    slabs, tranks, lranks = shape
    groups = tranks * lranks
    devices = slabs * groups
    rows = tiles.shape[0]
    lats, lons = lat_factor.shape[0], lon_factor.shape[0]
    lat_dev = lats // groups
    lon_pad = -(-lons // 16) * 16
    fields = V * time_factor.shape[0] * level_factor.shape[0]
    return [
        ((rows * BLK, LANES), jnp.float32),
        ((RC // BLK, lats, BLK), jnp.bfloat16),
        ((slabs, lats * (rows // slabs), LANES), jnp.float32),
        ((slabs, lats * (rows // slabs), LANES), jnp.bfloat16),
        ((slabs, rows // slabs, LANES), jnp.int32),
        ((lranks, slabs // lranks, lats * (rows // slabs), LANES), jnp.bfloat16),
        ((lranks, slabs // lranks, rows // slabs, LANES), jnp.int32),
        ((slabs, lons, RD // lranks), jnp.bfloat16),
        ((groups, lat_dev, rows, slabs * lon_pad), jnp.float32),
        ((groups, slabs, lon_pad, lat_dev * rows), jnp.bfloat16),
        ((devices, lon_pad, lat_dev * rows), jnp.bfloat16),
        ((1, 4 * rows), jnp.int32),
        ((devices, 1, 4 * rows), jnp.int32),
        ((fields, devices * rows), jnp.bfloat16),
        ((fields // LANES, lat_dev * lon_pad, LANES), jnp.float32),
        (tiles.shape, jnp.bfloat16),
        ((3, 1, rows), jnp.int32),
        (time_factor.shape, jnp.bfloat16),
        (level_factor.shape, jnp.bfloat16),
        (lat_factor.shape, jnp.bfloat16),
    ]


def bytes_of(buffers):
    total = 0
    for dims, kind in buffers:
        size = jnp.dtype(kind).itemsize
        for d in dims[:-1]:
            size *= d
        total += size * (-(-dims[-1] // LANES) * LANES)
    return total


def per_device(
    tiles,
    tile_var,
    tile_time,
    tile_level,
    tile_block,
    counts,
    time_factor,
    level_factor,
    lat_factor,
    lon_factor,
):
    shape = tuple(lax.axis_size(name) for name in ("slab", "trank", "lrank"))
    slabs = shape[0]
    devices = shape[0] * shape[1] * shape[2]
    rows = tiles.shape[0]
    fields = V * time_factor.shape[0] * level_factor.shape[0]
    buffers = scratch_of(shape, tiles, time_factor, level_factor, lat_factor, lon_factor)
    fits = (
        4 * rows == LANES
        and rows // slabs == 8
        and slabs % shape[2] == 0
        and (RD // slabs) % LANES == 0
        and fields % LANES == 0
        and bytes_of(buffers) < (24 << 20)
    )
    if not fits:
        return general_plan(
            tiles,
            tile_var,
            tile_time,
            tile_level,
            tile_block,
            counts,
            time_factor,
            level_factor,
            lat_factor,
            lon_factor,
        )
    lat_dev = lat_factor.shape[0] // (devices // slabs)
    in_vmem = pl.BlockSpec(memory_space=pltpu.VMEM)
    in_hbm = pl.BlockSpec(memory_space=pltpu.HBM)
    return pl.pallas_call(
        functools.partial(decode_kernel, shape),
        out_shape=jax.ShapeDtypeStruct((lon_factor.shape[0], lat_dev, fields), jnp.bfloat16),
        in_specs=[in_hbm] * 10,
        out_specs=in_vmem,
        scratch_shapes=[pltpu.VMEM(dims, kind) for dims, kind in buffers]
        + [
            pltpu.SMEM((rows,), jnp.int32),
            pltpu.SMEM((1, slabs), jnp.int32),
            pltpu.SemaphoreType.DMA((10,)),
        ]
        + [pltpu.SemaphoreType.DMA((slabs,))] * 2
        + [pltpu.SemaphoreType.DMA((shape[2],))] * 4
        + [pltpu.SemaphoreType.DMA((devices - 1,))] * 4,
        compiler_params=pltpu.CompilerParams(collective_id=0, has_side_effects=True),
        name="decode",
    )(
        tiles,
        tile_var.reshape(1, rows),
        tile_time.reshape(1, rows),
        tile_level.reshape(1, rows),
        tile_block,
        counts,
        time_factor,
        level_factor,
        lat_factor,
        lon_factor,
    )


def solution(mesh):
    in_specs = (
        P(("week", "slab", "trank", "lrank"), None),
        P(("week", "slab", "trank", "lrank")),
        P(("week", "slab", "trank", "lrank")),
        P(("week", "slab", "trank", "lrank")),
        P(("week", "slab", "trank", "lrank")),
        P(("week", "slab", "trank", "lrank"), None),
        P("week", None),
        P("week", None),
        P("week", None),
        P(("week", "slab"), None),
    )
    out_specs = P(("week", "slab"), ("trank", "lrank"), None)
    return jax.shard_map(
        per_device, mesh=mesh, in_specs=in_specs, out_specs=out_specs, check_vma=False
    )
```

```python
import functools

import jax
import jax.numpy as jnp
from jax import lax
from jax.experimental import pallas as pl
from jax.experimental.pallas import tpu as pltpu
from jax.sharding import PartitionSpec as P

V = 6
RT = 256
RL = 96
RC = 512
RD = 2048
BLK = 64


def general_plan(
    tiles,
    tile_var,
    tile_time,
    tile_level,
    tile_block,
    counts,
    time_factor,
    level_factor,
    lat_factor,
    lon_factor,
):
    slabs = lax.axis_size("slab")
    n_trank = lax.axis_size("trank")
    n_lrank = lax.axis_size("lrank")
    slots = tiles.shape[0]
    capacity = slots // slabs
    lat_rows = lat_factor.shape[0]
    cblocks = RC // BLK
    dblocks = RD // (BLK * slabs)
    time_dev = RT // n_trank
    level_dev = RL // n_lrank
    hours = time_factor.shape[0]
    levels = level_factor.shape[0]
    fields = V * hours * levels
    lat_blocks = lat_factor.reshape(lat_rows, cblocks, BLK)
    sent_counts = counts.reshape(slabs)
    slot_index = jnp.arange(slots, dtype=jnp.int32)
    live_sent = (slot_index % capacity < jnp.repeat(sent_counts, capacity)).astype(jnp.int32)
    got_tiles, variable, rank_time, rank_level, blocks, live_got = (
        lax.all_to_all(tiles, "slab", split_axis=0, concat_axis=0, tiled=True),
        lax.all_to_all(tile_var, "slab", split_axis=0, concat_axis=0, tiled=True),
        lax.all_to_all(tile_time, "slab", split_axis=0, concat_axis=0, tiled=True),
        lax.all_to_all(tile_level, "slab", split_axis=0, concat_axis=0, tiled=True),
        lax.all_to_all(tile_block, "slab", split_axis=0, concat_axis=0, tiled=True),
        lax.all_to_all(live_sent, "slab", split_axis=0, concat_axis=0, tiled=True),
    )
    chosen = jnp.take(lat_blocks, blocks // dblocks, axis=1)
    square = got_tiles.reshape(got_tiles.shape[0], BLK, BLK)
    product = jnp.einsum("lkc,kcd->kld", chosen, square, preferred_element_type=jnp.float32)
    partial_value = product.astype(jnp.bfloat16)
    time_full = lax.axis_index("trank") * time_dev + rank_time
    level_full = lax.axis_index("lrank") * level_dev + rank_level
    var_hot = (variable[:, None] == jnp.arange(V, dtype=jnp.int32)[None, :]).astype(jnp.float32)
    time_cols = jnp.take(time_factor, time_full, axis=1).T.astype(jnp.float32)
    level_cols = jnp.take(level_factor, level_full, axis=1).T.astype(jnp.float32)
    coef = var_hot[:, :, None, None] * time_cols[:, None, :, None] * level_cols[:, None, None, :]
    coef = coef * live_got.astype(jnp.float32)[:, None, None, None]
    coef = coef.reshape(variable.shape[0], fields).astype(jnp.bfloat16)
    place = (blocks % dblocks)[:, None] == jnp.arange(dblocks, dtype=jnp.int32)[None, :]
    spread_spread = jnp.where(
        place[:, None, :, None], partial_value[:, :, None, :], jnp.zeros((), jnp.bfloat16)
    )
    spread = spread_spread.reshape(partial_value.shape[0], partial_value.shape[1], dblocks * BLK)
    summed = lax.psum_scatter(
        jnp.einsum("kld,kx->ldx", spread, coef, preferred_element_type=jnp.float32).astype(
            jnp.bfloat16
        ),
        ("trank", "lrank"),
        scatter_dimension=0,
        tiled=True,
    )
    grid = jnp.einsum(
        "od,ldx->olx",
        lon_factor,
        lax.all_gather(summed, "slab", axis=1, tiled=True),
        preferred_element_type=jnp.float32,
    )
    return grid.astype(jnp.bfloat16)


LANES = 128
MESH = pl.DeviceIdType.MESH


def offsets(shape):
    slabs, tranks, lranks = shape
    found = [
        (a, b, c)
        for a in range(slabs)
        for b in range(tranks)
        for c in range(lranks)
        if (a, b, c) != (0, 0, 0)
    ]
    return sorted(found, key=lambda k: -(min(k[0], slabs - k[0]) * 4 + k[1] * 2 + k[2]))


def decode_kernel(
    shape,
    tiles_hbm,
    var_hbm,
    time_hbm,
    level_hbm,
    blk_hbm,
    counts_hbm,
    time_factor_hbm,
    level_factor_hbm,
    lat_hbm,
    lon_hbm,
    out_ref,
    square,
    lat_blocks,
    partials,
    stage,
    stage_place,
    got_part,
    got_place,
    lon_all,
    weights,
    send_buf,
    recv_buf,
    meta_mine,
    meta_all,
    coef,
    result,
    tiles_ref,
    index_ref,
    time_factor_ref,
    level_factor_ref,
    lat_ref,
    blk_ref,
    counts_ref,
    load_sem,
    lon_send,
    lon_recv,
    part_send,
    part_recv,
    place_send,
    place_recv,
    meta_send,
    meta_recv,
    w_send,
    w_recv,
):
    slabs, tranks, lranks = shape
    groups = tranks * lranks
    devices = slabs * groups
    week = lax.axis_index("week")
    slab = lax.axis_index("slab")
    trank = lax.axis_index("trank")
    lrank = lax.axis_index("lrank")
    me = slab * groups + trank * lranks + lrank
    rows = tiles_ref.shape[0]
    capacity = rows // slabs
    lats = lat_ref.shape[0]
    lat_dev = lats // groups
    lons, lon_pad = lon_hbm.shape[0], recv_buf.shape[1]
    own = slabs // lranks
    own_rows = own * capacity
    depth = RD // slabs
    dblocks = depth // BLK
    per_lane = LANES // BLK
    hours = time_factor_ref.shape[0]
    levels = level_factor_ref.shape[0]
    time_dev = RT // tranks
    level_dev = RL // lranks
    total_rows = rows * devices
    pieces = offsets(shape)

    def peer(k):
        a, b, c = k
        return (
            lax.rem(slab + a, slabs),
            lax.rem(trank + b, tranks),
            lax.rem(lrank + c, lranks),
        )

    orders = [sorted(range(slabs), key=lambda t: -abs(t - at)) for at in range(slabs)]
    line = []
    for n in range(slabs):
        target = jnp.int32(orders[0][n])
        for at in range(1, slabs):
            target = jnp.where(slab == at, orders[at][n], target)
        line.append(target)

    barrier = pltpu.get_barrier_semaphore()
    for k in pieces:
        pl.semaphore_signal(barrier, inc=1, device_id=(week, *peer(k)), device_id_type=MESH)
    columns = pl.ds(pl.multiple_of(lrank * (own * depth), own * depth), own * depth)
    loads = [
        pltpu.make_async_copy(src, dst, load_sem.at[n])
        for n, (src, dst) in enumerate(
            [
                (tiles_hbm, tiles_ref),
                (lat_hbm, lat_ref),
                (blk_hbm, blk_ref),
                (counts_hbm, counts_ref),
                (var_hbm, index_ref.at[0]),
                (time_hbm, index_ref.at[1]),
                (level_hbm, index_ref.at[2]),
                (time_factor_hbm, time_factor_ref),
                (level_factor_hbm, level_factor_ref),
                (lon_hbm.at[:, columns], lon_all.at[slab]),
            ]
        )
    ]
    for load in loads:
        load.start()
    for load in loads:
        load.wait()

    lane = lax.broadcasted_iota(jnp.int32, (1, rows), 1)
    live = jnp.zeros((1, rows), jnp.int32)
    for e in range(slabs):
        first = e * capacity
        live = jnp.where((lane >= first) & (lane < first + counts_ref[0, e]), 1, live)
    meta_mine[...] = jnp.concatenate(
        [
            index_ref[0],
            index_ref[1] + trank * time_dev,
            index_ref[2] + lrank * level_dev,
            live,
        ],
        axis=1,
    )
    pl.semaphore_wait(barrier, devices - 1)

    lon_copies = []
    for to_slab in line[:-1]:
        a = lax.rem(to_slab - slab + slabs, slabs)
        lon_copies.append(
            pltpu.make_async_remote_copy(
                src_ref=lon_hbm.at[:, columns],
                dst_ref=lon_all.at[slab],
                send_sem=lon_send.at[a],
                recv_sem=lon_recv.at[a],
                device_id=(week, to_slab, trank, lrank),
                device_id_type=MESH,
            )
        )
        lon_copies[-1].start()
    meta_copies = []
    for n, k in enumerate(pieces):
        meta_copies.append(
            pltpu.make_async_remote_copy(
                src_ref=meta_mine,
                dst_ref=meta_all.at[me],
                send_sem=meta_send.at[n],
                recv_sem=meta_recv.at[n],
                device_id=(week, *peer(k)),
                device_id_type=MESH,
            )
        )
        meta_copies[-1].start()
    meta_all[me] = meta_mine[...]

    half = lax.broadcasted_iota(jnp.int32, (rows, LANES), 1) < BLK
    for j in range(BLK // per_lane):
        chunk = tiles_ref[:, j * LANES : (j + 1) * LANES].astype(jnp.float32)
        turned = pltpu.roll(chunk, BLK, 1)
        square[pl.ds(per_lane * j, rows, stride=BLK), :] = jnp.where(half, chunk, turned)
        square[pl.ds(per_lane * j + 1, rows, stride=BLK), :] = jnp.where(half, turned, chunk)
    for cb in range(RC // BLK):
        lat_blocks[cb] = lat_ref[:, cb * BLK : (cb + 1) * BLK]
    for r in range(rows):
        e, q = r // capacity, r % capacity
        partials[e, pl.ds(q, lats, stride=capacity), :] = jnp.dot(
            lat_blocks[blk_ref[r] // dblocks],
            square[r * BLK : (r + 1) * BLK, :].astype(jnp.bfloat16),
            preferred_element_type=jnp.float32,
        )

    sub = lax.broadcasted_iota(jnp.int32, (capacity, LANES), 0)
    side = lax.broadcasted_iota(jnp.int32, (capacity, LANES), 1) // BLK
    for e in range(slabs):
        place = jnp.zeros((capacity, LANES), jnp.int32)
        for q in range(capacity):
            place = jnp.where(sub == q, blk_ref[e * capacity + q] % dblocks, place)
        stage_place[e] = place
    stage[...] = partials[...].astype(jnp.bfloat16)

    part_copies = []
    for c in range(1, lranks):
        other = lax.rem(lrank + c, lranks)
        theirs = pl.ds(other * own, own)
        for src, dst, send, recv in (
            (stage, got_part, part_send, part_recv),
            (stage_place, got_place, place_send, place_recv),
        ):
            part_copies.append(
                pltpu.make_async_remote_copy(
                    src_ref=src.at[theirs],
                    dst_ref=dst.at[lrank],
                    send_sem=send.at[c],
                    recv_sem=recv.at[c],
                    device_id=(week, slab, trank, other),
                    device_id_type=MESH,
                )
            )
            part_copies[-1].start()
    got_part[lrank] = stage[pl.ds(lrank * own, own)]
    got_place[lrank] = stage_place[pl.ds(lrank * own, own)]
    for copy in part_copies:
        copy.wait()

    for copy in lon_copies:
        copy.wait()
    blank = jnp.zeros((slabs, lon_pad - lons, depth), jnp.float32)
    for e in range(own):
        longitudes = jnp.concatenate(
            [lon_all[:, :, e * depth : (e + 1) * depth].astype(jnp.float32), blank], axis=1
        ).reshape(slabs * lon_pad, depth).astype(jnp.bfloat16)
        for source in range(lranks):
            place = got_place[source, e]
            part = got_part[source, e].astype(jnp.float32).reshape(lats, capacity, LANES)
            spread = jnp.concatenate(
                [
                    jnp.where((place == per_lane * b + side)[None], part, 0.0)
                    for b in range(dblocks // per_lane)
                ],
                axis=2,
            ).reshape(lats * capacity, depth).astype(jnp.bfloat16)
            value = lax.dot_general(
                spread, longitudes, (((1,), (1,)), ((), ())), preferred_element_type=jnp.float32
            )
            first = source * own_rows + e * capacity
            weights[:, :, first : first + capacity, :] = value.reshape(
                groups, lat_dev, capacity, slabs * lon_pad
            )
    for g in range(groups):
        turned = weights[g].reshape(lat_dev * rows, slabs * lon_pad).T
        send_buf[g] = turned.astype(jnp.bfloat16).reshape(slabs, lon_pad, lat_dev * rows)

    w_copies = []
    around = sorted(
        [(b, c) for b in range(tranks) for c in range(lranks)], key=lambda k: -(k[0] * 2 + k[1])
    )
    for n, to_slab in enumerate(line):
        for b, c in around:
            if n == slabs - 1 and (b, c) == (0, 0):
                continue
            _, to_trank, to_lrank = peer((0, b, c))
            way = lax.rem(to_slab - slab + slabs, slabs) * groups + b * lranks + c
            w_copies.append(
                pltpu.make_async_remote_copy(
                    src_ref=send_buf.at[to_trank * lranks + to_lrank, to_slab],
                    dst_ref=recv_buf.at[me],
                    send_sem=w_send.at[way],
                    recv_sem=w_recv.at[way],
                    device_id=(week, to_slab, to_trank, to_lrank),
                    device_id_type=MESH,
                )
            )
            w_copies[-1].start()
    recv_buf[me] = send_buf[trank * lranks + lrank, slab]

    for copy in meta_copies:
        copy.wait()

    def field(k):
        return jnp.concatenate(
            [
                meta_all[p * lranks + source][
                    :, k * rows + core * own_rows : k * rows + (core + 1) * own_rows
                ]
                for p in range(devices // lranks)
                for core in range(lranks)
                for source in range(lranks)
            ],
            axis=1,
        )

    variable, rank_time, rank_level, alive = field(0), field(1), field(2), field(3)
    time_hot = (
        lax.broadcasted_iota(jnp.int32, (RT, total_rows), 0) == rank_time
    ).astype(jnp.float32).astype(jnp.bfloat16)
    level_hot = (
        lax.broadcasted_iota(jnp.int32, (RL, total_rows), 0) == rank_level
    ).astype(jnp.float32).astype(jnp.bfloat16)
    time_f = time_factor_ref[...].astype(jnp.float32)
    time_rows = jnp.concatenate(
        [jnp.broadcast_to(time_f[t : t + 1], (levels, RT)) for t in range(hours)], axis=0
    ).astype(jnp.bfloat16)
    level_f = level_factor_ref[...].astype(jnp.float32)
    level_rows = jnp.concatenate([level_f] * hours, axis=0).astype(jnp.bfloat16)
    product = (
        jnp.dot(time_rows, time_hot, preferred_element_type=jnp.float32)
        * jnp.dot(level_rows, level_hot, preferred_element_type=jnp.float32)
        * alive.astype(jnp.float32)
    )
    per_var = hours * levels
    for v in range(V):
        coef[v * per_var : (v + 1) * per_var, :] = jnp.where(
            variable == v, product, 0.0
        ).astype(jnp.bfloat16)

    for copy in w_copies:
        copy.wait()

    got = [recv_buf[i].astype(jnp.float32) for i in range(devices)]
    left = jnp.concatenate(
        [
            jnp.concatenate([x[:, y * rows : (y + 1) * rows] for x in got], axis=1)
            for y in range(lat_dev)
        ],
        axis=0,
    ).astype(jnp.bfloat16)
    full = lax.dot_general(
        left, coef[...], (((1,), (1,)), ((), ())), preferred_element_type=jnp.float32
    )
    blocks = full.shape[1] // LANES
    for b in range(blocks):
        result[b] = full[:, b * LANES : (b + 1) * LANES]
    for o in range(lons):
        out_ref[o] = jnp.concatenate(
            [result[b, pl.ds(o, lat_dev, stride=lon_pad), :] for b in range(blocks)], axis=1
        ).astype(jnp.bfloat16)


def scratch_of(shape, tiles, time_factor, level_factor, lat_factor, lon_factor):
    slabs, tranks, lranks = shape
    groups = tranks * lranks
    devices = slabs * groups
    rows = tiles.shape[0]
    lats, lons = lat_factor.shape[0], lon_factor.shape[0]
    lat_dev = lats // groups
    lon_pad = -(-lons // 16) * 16
    fields = V * time_factor.shape[0] * level_factor.shape[0]
    return [
        ((rows * BLK, LANES), jnp.float32),
        ((RC // BLK, lats, BLK), jnp.bfloat16),
        ((slabs, lats * (rows // slabs), LANES), jnp.float32),
        ((slabs, lats * (rows // slabs), LANES), jnp.bfloat16),
        ((slabs, rows // slabs, LANES), jnp.int32),
        ((lranks, slabs // lranks, lats * (rows // slabs), LANES), jnp.bfloat16),
        ((lranks, slabs // lranks, rows // slabs, LANES), jnp.int32),
        ((slabs, lons, RD // lranks), jnp.bfloat16),
        ((groups, lat_dev, rows, slabs * lon_pad), jnp.float32),
        ((groups, slabs, lon_pad, lat_dev * rows), jnp.bfloat16),
        ((devices, lon_pad, lat_dev * rows), jnp.bfloat16),
        ((1, 4 * rows), jnp.int32),
        ((devices, 1, 4 * rows), jnp.int32),
        ((fields, devices * rows), jnp.bfloat16),
        ((fields // LANES, lat_dev * lon_pad, LANES), jnp.float32),
        (tiles.shape, jnp.bfloat16),
        ((3, 1, rows), jnp.int32),
        (time_factor.shape, jnp.bfloat16),
        (level_factor.shape, jnp.bfloat16),
        (lat_factor.shape, jnp.bfloat16),
    ]


def bytes_of(buffers):
    total = 0
    for dims, kind in buffers:
        size = jnp.dtype(kind).itemsize
        for d in dims[:-1]:
            size *= d
        total += size * (-(-dims[-1] // LANES) * LANES)
    return total


def per_device(
    tiles,
    tile_var,
    tile_time,
    tile_level,
    tile_block,
    counts,
    time_factor,
    level_factor,
    lat_factor,
    lon_factor,
):
    shape = tuple(lax.axis_size(name) for name in ("slab", "trank", "lrank"))
    slabs = shape[0]
    devices = shape[0] * shape[1] * shape[2]
    rows = tiles.shape[0]
    fields = V * time_factor.shape[0] * level_factor.shape[0]
    buffers = scratch_of(shape, tiles, time_factor, level_factor, lat_factor, lon_factor)
    fits = (
        4 * rows == LANES
        and rows // slabs == 8
        and slabs % shape[2] == 0
        and (RD // slabs) % LANES == 0
        and fields % LANES == 0
        and bytes_of(buffers) < (24 << 20)
    )
    if not fits:
        return general_plan(
            tiles,
            tile_var,
            tile_time,
            tile_level,
            tile_block,
            counts,
            time_factor,
            level_factor,
            lat_factor,
            lon_factor,
        )
    lat_dev = lat_factor.shape[0] // (devices // slabs)
    in_vmem = pl.BlockSpec(memory_space=pltpu.VMEM)
    in_hbm = pl.BlockSpec(memory_space=pltpu.HBM)
    hbm = lambda x: pltpu.with_memory_space_constraint(x, pltpu.HBM)
    return pl.pallas_call(
        functools.partial(decode_kernel, shape),
        out_shape=jax.ShapeDtypeStruct((lon_factor.shape[0], lat_dev, fields), jnp.bfloat16),
        in_specs=[in_hbm] * 10,
        out_specs=in_vmem,
        scratch_shapes=[pltpu.VMEM(dims, kind) for dims, kind in buffers]
        + [
            pltpu.SMEM((rows,), jnp.int32),
            pltpu.SMEM((1, slabs), jnp.int32),
            pltpu.SemaphoreType.DMA((10,)),
        ]
        + [pltpu.SemaphoreType.DMA((slabs,))] * 2
        + [pltpu.SemaphoreType.DMA((shape[2],))] * 4
        + [pltpu.SemaphoreType.DMA((devices,))] * 4,
        compiler_params=pltpu.CompilerParams(collective_id=0, has_side_effects=True, vmem_limit_bytes=16 << 20),
        name="decode",
    )(
        hbm(tiles),
        hbm(tile_var.reshape(1, rows)),
        hbm(tile_time.reshape(1, rows)),
        hbm(tile_level.reshape(1, rows)),
        hbm(tile_block),
        hbm(counts),
        hbm(time_factor),
        hbm(level_factor),
        hbm(lat_factor),
        hbm(lon_factor),
    )


def solution(mesh):
    in_specs = (
        P(("week", "slab", "trank", "lrank"), None),
        P(("week", "slab", "trank", "lrank")),
        P(("week", "slab", "trank", "lrank")),
        P(("week", "slab", "trank", "lrank")),
        P(("week", "slab", "trank", "lrank")),
        P(("week", "slab", "trank", "lrank"), None),
        P("week", None),
        P("week", None),
        P("week", None),
        P(("week", "slab"), None),
    )
    out_specs = P(("week", "slab"), ("trank", "lrank"), None)
    return jax.shard_map(
        per_device, mesh=mesh, in_specs=in_specs, out_specs=out_specs, check_vma=False
    )
```
